32 devices in a mesh: leaf: 8 (over z, y), row: 4 (over x, core).
Axes of the slice: x: 2, y: 2, z: 4, core: 2. Of those that a mesh axis runs over, the one named last changes fastest.
Arguments:
- panel0: float32 [12288, 512], P(('leaf', 'row')), may hold values from -3 to 30, as said below
- panel1: float32 [6144, 512], P(('leaf', 'row')), may hold values from -3 to 30
- panel2: float32 [3072, 512], P(('leaf', 'row')), may hold values from -3 to 30
- panel3: float32 [1536, 512], P(('leaf', 'row')), may hold values from -3 to 30
- maps1: int32 [8, 8], replicated, may hold values from 0 to 11, as said below
- maps2: int32 [4, 8], replicated, may hold values from 0 to 11, as said below
- maps3: int32 [2, 8], replicated, may hold values from 0 to 11, as said below
Outputs:
- update_top: float32 [1024, 1024], P(('leaf', 'row'))
The draws below stay inside these ranges and needn't reach their ends.
Inputs may be any that keep to these rules, and one draw needn't show every extreme that they name: `panel0`: each front's first 512 rows form a symmetric matrix, and every assembled pivot block is positive definite. `maps1`: each row lists distinct parent block numbers. `maps2`: each row lists distinct parent block numbers. `maps3`: each row lists distinct parent block numbers.
All inputs are finite; a program needn't handle non-finite values.
Results may differ from the reference program's by a relative error of at most 0.0003.
Values sent between devices are 32-bit elements; how exact they have to be, the bound alone decides.
A program may use at most 128 MiB of HBM per device.

```python
import math
import jax
import jax.numpy as jnp
from jax import lax

BLOCK = 128
PIV = 512
UPD = 1024
N_LEAF = 8


def draw_noise(key, shape):
    return jnp.clip(jax.random.normal(key, shape, jnp.float32), -4.0, 4.0)


def make_panels(key, front_count):
    keys = jax.random.split(key, 3)
    diagonal = jax.random.uniform(keys[0], (front_count, PIV), jnp.float32, 12.0, 24.0)
    raw = draw_noise(keys[1], (front_count, PIV, PIV)) * (3.6 / math.sqrt(PIV))
    pivot = (raw + jnp.swapaxes(raw, 1, 2)) / math.sqrt(2.0)
    pivot = pivot + diagonal[:, :, None] * jnp.eye(PIV, dtype=jnp.float32)[None, :, :]
    coupling = draw_noise(keys[2], (front_count, UPD, PIV)) * (3.0 / math.sqrt(PIV))
    stacked = jnp.concatenate([pivot, coupling], axis=1)
    return stacked.reshape(front_count * (PIV + UPD), PIV)


def make_maps(key, child_count):
    keys = jax.random.split(key, child_count)
    parent_blocks = (PIV + UPD) // BLOCK

    def one_row(one_key):
        return jax.random.permutation(one_key, parent_blocks)[:UPD // BLOCK]
    return jax.vmap(one_row)(keys).astype(jnp.int32)


def draw_panel0(key, part):
    return make_panels(jax.random.fold_in(key, 10), N_LEAF)


def draw_panel1(key, part):
    return make_panels(jax.random.fold_in(key, 11), N_LEAF // 2)


def draw_panel2(key, part):
    return make_panels(jax.random.fold_in(key, 12), N_LEAF // 4)


def draw_panel3(key, part):
    return make_panels(jax.random.fold_in(key, 13), N_LEAF // 8)


def draw_maps1(key, part):
    return make_maps(jax.random.fold_in(key, 21), N_LEAF)


def draw_maps2(key, part):
    return make_maps(jax.random.fold_in(key, 22), N_LEAF // 2)


def draw_maps3(key, part):
    return make_maps(jax.random.fold_in(key, 23), N_LEAF // 4)


def setup_inputs(seed: int = 0) -> dict:
    splits = jax.random.split(jax.random.key(seed), 8)
    panel0 = draw_panel0(jax.random.fold_in(splits[7], 71), 0)
    panel1 = draw_panel1(jax.random.fold_in(splits[7], 71), 0)
    panel2 = draw_panel2(jax.random.fold_in(splits[7], 71), 0)
    panel3 = draw_panel3(jax.random.fold_in(splits[7], 71), 0)
    maps1 = draw_maps1(jax.random.fold_in(splits[7], 71), 0)
    maps2 = draw_maps2(jax.random.fold_in(splits[7], 71), 0)
    maps3 = draw_maps3(jax.random.fold_in(splits[7], 71), 0)
    return {"panel0": panel0, "panel1": panel1, "panel2": panel2, "panel3": panel3, "maps1": maps1, "maps2": maps2, "maps3": maps3}


exact_mode = lax.Precision.HIGHEST

def extend_add(update, blocks):
    parent_blocks = (PIV + UPD) // BLOCK
    child_blocks = blocks.shape[0]
    onehot = (blocks[:, None] == jnp.arange(parent_blocks, dtype=jnp.int32)[None, :]).astype(jnp.float32)
    tile_grid = update.reshape(child_blocks, BLOCK, child_blocks, BLOCK)
    spread = jnp.einsum('ia,ixjy->axjy', onehot, tile_grid, precision=exact_mode)
    placed = jnp.einsum('axjy,jb->axby', spread, onehot, precision=exact_mode)
    return placed.reshape(parent_blocks * BLOCK, parent_blocks * BLOCK)

def factor_front(front_rows, trailing, upper_panel):
    assembled = front_rows + upper_panel
    factor = jnp.linalg.cholesky(assembled[:PIV])
    columns = lax.linalg.triangular_solve(factor, assembled[PIV:], left_side=False, lower=True, transpose_a=True)
    return trailing - jnp.dot(columns.astype(jnp.float32), columns.T.astype(jnp.float32), precision=exact_mode, preferred_element_type=jnp.float32)

def reference(panel0, panel1, panel2, panel3, maps1, maps2, maps3):
    front_size = PIV + UPD
    child_blocks = UPD // BLOCK
    fronts = panel0.reshape(N_LEAF, front_size, PIV)

    def leaf_front(front_rows):
        return factor_front(front_rows, jnp.zeros((UPD, UPD), jnp.float32), jnp.zeros((front_size, PIV), jnp.float32))
    schur = lax.map(leaf_front, fronts)
    level_index = 1
    for panel_rows, block_maps in ((panel1, maps1), (panel2, maps2), (panel3, maps3)):
        front_count = N_LEAF // 2 ** level_index
        fronts = panel_rows.reshape(front_count, front_size, PIV)
        children = schur.reshape(front_count, 2, UPD, UPD)
        map_pairs = block_maps.reshape(front_count, 2, child_blocks)

        def parent(inputs):
            front_rows, child_pair, map_pair = inputs
            upper = extend_add(child_pair[0], map_pair[0]) + extend_add(child_pair[1], map_pair[1])
            return factor_front(front_rows, upper[PIV:, PIV:], upper[:, :PIV])
        schur = lax.map(parent, (fronts, children, map_pairs))
        level_index = level_index + 1
    return schur.reshape(N_LEAF // 8 * UPD, UPD)
```

```python
import functools

import jax
import jax.numpy as jnp
from jax import lax
from jax.experimental import pallas as pl
from jax.experimental.pallas import tpu as pltpu
from jax.sharding import PartitionSpec as P

BLOCK = 128
SUB = 8
LEVELS = 4
CONTRACT_LAST = (((1,), (1,)), ((), ()))


def partner(block, axis, stride):
    count = lax.axis_size(axis)
    route = []
    for low in range(count):
        high = low | 1 << stride
        if high != low and high < count:
            route += [(low, high), (high, low)]
    return lax.ppermute(block, axis, route)


def halves(value):
    high = value.astype(jnp.bfloat16)
    low = (value - high.astype(jnp.float32)).astype(jnp.bfloat16)
    return high, low


def dot_split(left, right):
    left_high, left_low = left
    right_high, right_low = right

    def one(a, b):
        return lax.dot_general(a, b, CONTRACT_LAST, preferred_element_type=jnp.float32)

    return one(left_high, right_high) + (one(left_high, right_low) + one(left_low, right_high))


def dot_nt(left, right):
    return dot_split(halves(left), halves(right))


def spread(value, rows, columns):
    return jnp.broadcast_to(value, (rows, columns))


def diagonal_inverse(block):
    count = BLOCK // SUB
    rows = [block[v * SUB : (v + 1) * SUB] for v in range(count)]
    lane = lax.broadcasted_iota(jnp.int32, (SUB, BLOCK), 1)
    sub = lax.broadcasted_iota(jnp.int32, (SUB, BLOCK), 0)
    for b in range(count):
        base = b * SUB
        inside = (lane >= base) & (lane < base + SUB)
        own = rows[b]
        columns = [spread(own[:, base + j : base + j + 1], SUB, BLOCK) for j in range(SUB)]
        a = [
            [spread(columns[j][i : i + 1], SUB, BLOCK) for j in range(i + 1)] for i in range(SUB)
        ]
        inverse = []
        ratio = [[None] * SUB for _ in range(SUB)]
        for i in range(SUB):
            inverse.append(1.0 / a[i][i])
            for j in range(i + 1, SUB):
                ratio[j][i] = a[j][i] * inverse[i]
            for j in range(i + 1, SUB):
                for k in range(i + 1, j + 1):
                    a[j][k] = a[j][k] - ratio[j][i] * a[k][i]
        cleared = jnp.where(inside, 0.0, own)
        pivots = []
        for j in range(SUB):
            row = spread(cleared[j : j + 1], SUB, BLOCK)
            row = jnp.where(lane == base + j, 1.0, row)
            for i in range(j):
                row = row - ratio[j][i] * pivots[i]
            pivots.append(row)
        for v in range(b + 1, count):
            old = rows[v]
            new = jnp.where(inside, 0.0, old)
            factors = []
            for j in range(SUB):
                column = spread(old[:, base + j : base + j + 1], SUB, BLOCK)
                for i in range(j):
                    column = column - factors[i] * a[j][i]
                factors.append(column * inverse[j])
            for j in range(SUB):
                new = new - factors[j] * pivots[j]
            rows[v] = new
        final = jnp.zeros((SUB, BLOCK), jnp.float32)
        scale = jnp.ones((SUB, BLOCK), jnp.float32)
        for j in range(SUB):
            final = jnp.where(sub == j, pivots[j], final)
            scale = jnp.where(sub == j, a[j][j], scale)
        rows[b] = jnp.where(lane <= sub + base, final / jnp.sqrt(scale), 0.0)
    return jnp.concatenate(rows, axis=0)


def factor(work, out):
    order = work.shape[0]
    tiles = order // BLOCK
    row_ids = lax.broadcasted_iota(jnp.int32, (order, BLOCK), 0)

    def step(j, carry):
        start = pl.multiple_of(j * BLOCK, BLOCK)
        span = pl.ds(start, BLOCK)
        inverse = diagonal_inverse(work[span, span])
        below = jnp.where(row_ids >= start + BLOCK, work[:, span], 0.0)
        column = dot_nt(below, inverse)
        out[:, span] = column
        out[span, span] = inverse
        pieces = halves(column)
        work[...] = work[...] - dot_split(pieces, pieces)
        return carry

    lax.fori_loop(0, tiles, step, 0)


def solve_below(factors, columns):
    order = factors.shape[0]
    for j in range(order // BLOCK):
        span = slice(j * BLOCK, (j + 1) * BLOCK)
        value = columns[:, span]
        if j:
            value = value - dot_nt(columns[:, : j * BLOCK], factors[span, : j * BLOCK])
        columns[:, span] = dot_nt(value, factors[span, span])


def front_kernel(level, row_count, *refs):
    last = level == LEVELS - 1
    group = 2**level
    if level == 0:
        info, inverse_map, gathered, *rest = refs
        old = None
    else:
        info, inverse_map, gathered, old, *rest = refs
    if last:
        out, work, factors, columns = rest
    else:
        if level == LEVELS - 2:
            kept, share, extra, work, factors, columns, placed = rest
        else:
            kept, share, work, factors, columns, placed = rest
    front, order = gathered.shape
    chunk = front // (row_count * group)
    below = front - order
    for member in range(group):
        for r in range(row_count):
            source = (r * group + member) * chunk
            target = (member * row_count + r) * chunk
            first = max(0, min(chunk, order - target))
            if first:
                work[target : target + first] = gathered[source : source + first]
            if first < chunk:
                low = target + first - order
                columns[low : low + chunk - first] = gathered[source + first : source + chunk]
    factor(work, factors)
    solve_below(factors, columns)
    if last:
        rows = out.shape[0]
        position = info[0] * row_count + info[1]
        mine = columns[pl.ds(pl.multiple_of(position * rows, 8), rows)]
        out[...] = dot_nt(mine, columns[...])
        return
    depth = 0 if old is None else old.shape[1]
    width = order // group
    if old is not None:
        kept[:below, :depth] = old[:below]
    offset = pl.multiple_of(info[0] % group * width, BLOCK)
    kept[:below, depth:] = columns[:, pl.ds(offset, width)]
    kept[below:] = jnp.zeros((BLOCK, depth + width), jnp.float32)
    for i in range(front // BLOCK):
        block = pl.multiple_of(inverse_map[i] * BLOCK, BLOCK)
        placed[i * BLOCK : (i + 1) * BLOCK] = kept[pl.ds(block, BLOCK)]
    pivots = halves(placed[:order])
    small = chunk // 2
    for member in range(2 * group):
        start = pl.multiple_of((member * row_count + info[1]) * small, 8)
        piece = halves(placed[pl.ds(start, small)])
        share[member * small : (member + 1) * small] = -dot_split(piece, pivots)
    kept[:below] = placed[order:]
    if level == LEVELS - 2:
        top = 2 * group
        rows = below // (top * row_count)
        full = halves(placed[order:])
        for member in range(top):
            start = pl.multiple_of(order + (member * row_count + info[1]) * rows, 8)
            piece = halves(placed[pl.ds(start, rows)])
            extra[member * rows : (member + 1) * rows] = -dot_split(piece, full)


def front_step(level, info, inverse_map, gathered, old, row_count):
    front, order = gathered.shape
    below = front - order
    depth = 0 if old is None else old.shape[1]
    width = order // 2**level
    float32 = jnp.float32
    scratch = [
        pltpu.VMEM((order, order), float32),
        pltpu.VMEM((order, order), float32),
        pltpu.VMEM((below, order), float32),
    ]
    if level == LEVELS - 1:
        rows = below // (2**level * row_count)
        shapes = jax.ShapeDtypeStruct((rows, below), float32)
    else:
        shapes = [
            jax.ShapeDtypeStruct((below + BLOCK, depth + width), float32),
            jax.ShapeDtypeStruct((front // row_count, order), float32),
        ]
        scratch.append(pltpu.VMEM((front, depth + width), float32))
        if level == LEVELS - 2:
            shapes.append(jax.ShapeDtypeStruct((below // row_count, below), float32))
    operands = [info, inverse_map, gathered]
    specs = [pl.BlockSpec(memory_space=pltpu.SMEM)] * 2 + [pl.BlockSpec(memory_space=pltpu.VMEM)]
    if old is not None:
        operands.append(old)
        specs.append(pl.BlockSpec(memory_space=pltpu.VMEM))
    return pl.pallas_call(
        functools.partial(front_kernel, level, row_count),
        out_shape=shapes,
        in_specs=specs,
        scratch_shapes=scratch,
        name=f"front{level}",
        compiler_params=pltpu.CompilerParams(vmem_limit_bytes=60 * 2**20),
    )(*operands)


def body(panel0, panel1, panel2, panel3, maps1, maps2, maps3):
    panels = (panel0, panel1, panel2, panel3)
    block_maps = (maps1, maps2, maps3)
    row_count = lax.axis_size("row")
    leaf = lax.axis_index("leaf")
    row = lax.axis_index("row")
    order = panel0.shape[1]
    front = panel0.shape[0] * row_count
    parents = front // BLOCK
    children = (front - order) // BLOCK
    old = None
    share = panel0
    extra = None
    for level in range(LEVELS):
        group = 2**level
        member = leaf % group
        if level:
            rows = panels[level].shape[0]
            start = member * rows
            mine = lax.dynamic_slice_in_dim(share, start, rows, 0) + panels[level]
            share = lax.dynamic_update_slice_in_dim(share, mine, start, 0)
            for bit in range(level):
                share = share + partner(share, "leaf", bit)
        gathered = lax.all_gather(share, "row", axis=0, tiled=True)
        info = jnp.stack([member, row]).astype(jnp.int32)
        if level < LEVELS - 1:
            blocks = lax.dynamic_index_in_dim(block_maps[level], leaf // group, 0, keepdims=False)
            hit = blocks[None, :] == jnp.arange(parents, dtype=jnp.int32)[:, None]
            back = jnp.min(
                jnp.where(hit, jnp.arange(children, dtype=jnp.int32)[None, :], children), axis=1
            )
        else:
            back = jnp.zeros((parents,), jnp.int32)
        result = front_step(level, info, back, gathered, old, row_count)
        if level == LEVELS - 1:
            product = result
        elif level == LEVELS - 2:
            old, share, extra = result
        else:
            old, share = result
    current = extra.reshape(2 ** (LEVELS - 1), -1, extra.shape[1])
    for bit in reversed(range(LEVELS - 1)):
        half = current.shape[0] // 2
        upper = leaf // 2**bit % 2
        kept = lax.dynamic_slice_in_dim(current, upper * half, half, 0)
        given = lax.dynamic_slice_in_dim(current, (1 - upper) * half, half, 0)
        current = kept + partner(given, "leaf", bit)
    return current[0] - product


def solution(mesh):
    rows = P(("leaf", "row"), None)
    return jax.shard_map(
        body,
        mesh=mesh,
        in_specs=(rows, rows, rows, rows, P(), P(), P()),
        out_specs=rows,
        check_vma=False,
    )
```

```python
import functools

import jax
import jax.numpy as jnp
from jax import lax
from jax.experimental import pallas as pl
from jax.experimental.pallas import tpu as pltpu
from jax.sharding import PartitionSpec as P

BLOCK = 128
SUB = 8
LEVELS = 4
CONTRACT_LAST = (((1,), (1,)), ((), ()))


def halves(value):
    high = value.astype(jnp.bfloat16)
    low = (value - high.astype(jnp.float32)).astype(jnp.bfloat16)
    return high, low


def dot_split(left, right):
    left_high, left_low = left
    right_high, right_low = right

    def one(a, b):
        return lax.dot_general(a, b, CONTRACT_LAST, preferred_element_type=jnp.float32)

    return one(left_high, right_high) + (one(left_high, right_low) + one(left_low, right_high))


def dot_nt(left, right):
    return dot_split(halves(left), halves(right))


def spread(value, rows, columns):
    return jnp.broadcast_to(value, (rows, columns))


def diagonal_inverse(block):
    count = BLOCK // SUB
    rows = [block[v * SUB : (v + 1) * SUB] for v in range(count)]
    lane = lax.broadcasted_iota(jnp.int32, (SUB, BLOCK), 1)
    sub = lax.broadcasted_iota(jnp.int32, (SUB, BLOCK), 0)
    for b in range(count):
        base = b * SUB
        inside = (lane >= base) & (lane < base + SUB)
        own = rows[b]
        columns = [spread(own[:, base + j : base + j + 1], SUB, BLOCK) for j in range(SUB)]
        a = [
            [spread(columns[j][i : i + 1], SUB, BLOCK) for j in range(i + 1)] for i in range(SUB)
        ]
        inverse = []
        ratio = [[None] * SUB for _ in range(SUB)]
        for i in range(SUB):
            inverse.append(1.0 / a[i][i])
            for j in range(i + 1, SUB):
                ratio[j][i] = a[j][i] * inverse[i]
            for j in range(i + 1, SUB):
                for k in range(i + 1, j + 1):
                    a[j][k] = a[j][k] - ratio[j][i] * a[k][i]
        cleared = jnp.where(inside, 0.0, own)
        pivots = []
        for j in range(SUB):
            row = spread(cleared[j : j + 1], SUB, BLOCK)
            row = jnp.where(lane == base + j, 1.0, row)
            for i in range(j):
                row = row - ratio[j][i] * pivots[i]
            pivots.append(row)
        for v in range(b + 1, count):
            old = rows[v]
            new = jnp.where(inside, 0.0, old)
            factors = []
            for j in range(SUB):
                column = spread(old[:, base + j : base + j + 1], SUB, BLOCK)
                for i in range(j):
                    column = column - factors[i] * a[j][i]
                factors.append(column * inverse[j])
            for j in range(SUB):
                new = new - factors[j] * pivots[j]
            rows[v] = new
        final = jnp.zeros((SUB, BLOCK), jnp.float32)
        scale = jnp.ones((SUB, BLOCK), jnp.float32)
        for j in range(SUB):
            final = jnp.where(sub == j, pivots[j], final)
            scale = jnp.where(sub == j, a[j][j], scale)
        rows[b] = jnp.where(lane <= sub + base, final / jnp.sqrt(scale), 0.0)
    return jnp.concatenate(rows, axis=0)


def factor(work, out, between):
    order = work.shape[0]
    tiles = order // BLOCK
    row_ids = lax.broadcasted_iota(jnp.int32, (order, BLOCK), 0)

    def step(j, carry):
        between(j)
        start = pl.multiple_of(j * BLOCK, BLOCK)
        span = pl.ds(start, BLOCK)
        inverse = diagonal_inverse(work[span, span])
        below = jnp.where(row_ids >= start + BLOCK, work[:, span], 0.0)
        column = dot_nt(below, inverse)
        out[:, span] = column
        out[span, span] = inverse
        pieces = halves(column)
        work[...] = work[...] - dot_split(pieces, pieces)
        return carry

    lax.fori_loop(0, tiles, step, 0)


def solve_below(factors, columns):
    order = factors.shape[0]
    for j in range(order // BLOCK):
        span = slice(j * BLOCK, (j + 1) * BLOCK)
        value = columns[:, span]
        if j:
            value = value - dot_nt(columns[:, : j * BLOCK], factors[span, : j * BLOCK])
        columns[:, span] = dot_nt(value, factors[span, span])


def neighbours(level):
    leaf = lax.axis_index("leaf")
    row = lax.axis_index("row")
    partners = []
    for bit in range(level):
        flag = leaf // 2**bit % 2
        partners.append({"leaf": leaf + (1 - 2 * flag) * 2**bit, "row": row})
    count = lax.axis_size("row")
    sibling = row + 1 - 2 * (row % 2)
    forward = [lax.rem(row + 2 * d, count) for d in range(1, count // 2)]
    backward = [lax.rem(row + count - 2 * d, count) for d in range(1, count // 2)]
    across = [{"leaf": leaf, "row": other} for other in forward]
    return partners, {"leaf": leaf, "row": sibling}, across, backward


def remote(source, target, sends, receives, slot, device):
    return pltpu.make_async_remote_copy(
        src_ref=source,
        dst_ref=target,
        send_sem=sends.at[slot],
        recv_sem=receives.at[slot],
        device_id=device,
        device_id_type=pl.DeviceIdType.MESH,
    )


class Gather:
    def __init__(self, buffer, place, sends, receives, slot, near):
        _, sibling, across, origins = near
        own = buffer.at[place(lax.axis_index("row"))]
        self.direct = remote(own, own, sends, receives, slot, sibling)
        self.far = []
        self.relay = []
        for n, (device, origin) in enumerate(zip(across, origins)):
            self.far.append(remote(own, own, sends, receives, slot + 1 + 2 * n, device))
            passed = buffer.at[place(origin)]
            self.relay.append(remote(passed, passed, sends, receives, slot + 2 + 2 * n, sibling))

    def start(self):
        for copy in self.far:
            copy.start()
        self.direct.start()

    def pass_on(self):
        for copy, relay in zip(self.far, self.relay):
            copy.wait_recv()
            relay.start()

    def finish(self):
        self.direct.wait_recv()
        for relay in self.relay:
            relay.wait_recv()
        for copy in [self.direct] + self.far + self.relay:
            copy.wait_send()


def rows_at(size, base=0):
    def place(row):
        return pl.ds(pl.multiple_of(row * size + base, 8), size)

    return place


def lower_tiles(order):
    return [(i, j) for i in range(order // BLOCK) for j in range(i + 1)]


def entry_barrier(near):
    partners, sibling, across, _ = near
    barrier = pltpu.get_barrier_semaphore()
    peers = partners + [sibling] + across
    for peer in peers:
        pl.semaphore_signal(barrier, inc=1, device_id=peer, device_id_type=pl.DeviceIdType.MESH)
    pl.semaphore_wait(barrier, len(peers))


def bit_reversed(index, bits):
    return sum((index >> b & 1) << (bits - 1 - b) for b in range(bits))


def front_kernel(level, row_count, front, order, *refs):
    last = level == LEVELS - 1
    first = level == 0
    group = 2**level
    below = front - order
    refs = list(refs)
    take = lambda: refs.pop(0)
    row = lax.axis_index("row")
    member = lax.axis_index("leaf") % group
    if first:
        panel = take()
    else:
        pivot_share, below_share = take(), take()
    if last:
        extra_in = take()
        out = take()
    else:
        fresh = take()
    work, factors, columns, sends, receives = take(), take(), take(), take(), take()
    near = neighbours(level)
    partners = near[0]
    tiles = lower_tiles(order)
    entry_barrier(near)
    if first:
        gathered = take()
        chunk = panel.shape[0]
        pieces = 3
        size = chunk // pieces
        own = pl.ds(pl.multiple_of(row * chunk, 8), chunk)
        gathered[own] = panel[...]
        moves = []
        for c in range(pieces):
            moves.append(Gather(gathered, rows_at_scaled(chunk, c * size, size), sends, receives, (row_count - 1) * c, near))
        for move in moves:
            move.start()
        for move in moves:
            move.pass_on()
        for move in moves:
            move.finish()
        work[...] = gathered[:order]
        columns[...] = gathered[order:]
        factor(work, factors, lambda j: None)
    else:
        packed, pivot_sum, pivot_in, below_sum, below_in = take(), take(), take(), take(), take()
        share = pivot_share.shape[0]
        mine = rows_at(share)(row)
        slot = 0
        source = pivot_share
        for bit in range(level):
            move = remote(source, pivot_in.at[bit], sends, receives, slot, partners[bit])
            slot += 1
            move.start()
            move.wait()
            total = source[...] + pivot_in[bit]
            if bit + 1 < level:
                pivot_sum[bit] = total
                source = pivot_sum.at[bit]
            else:
                packed[mine] = total
        spread_pivots = Gather(packed, rows_at(share), sends, receives, slot, near)
        slot += row_count - 1
        spread_pivots.start()
        chunks = 2
        piece = below_share.shape[0] // chunks
        orders = [list(range(level)), list(range(level))]
        if level > 1:
            orders[1][0], orders[1][1] = 1, 0
        moves = [[None] * level for _ in range(chunks)]
        spreads = []
        for c in range(chunks):
            for k in range(level):
                source = below_share.at[pl.ds(c * piece, piece)] if k == 0 else below_sum.at[c, k - 1]
                moves[c][k] = remote(
                    source, below_in.at[c, k], sends, receives, slot, partners[orders[c][k]]
                )
                slot += 1
            spreads.append(
                Gather(columns, rows_at_scaled(below_share.shape[0], c * piece, piece), sends, receives, slot, near)
            )
            slot += row_count - 1

        def advance(c, k):
            if k < level:
                moves[c][k].wait()
                if k == 0:
                    total = below_share[c * piece : (c + 1) * piece] + below_in[c, 0]
                else:
                    total = below_sum[c, k - 1] + below_in[c, k]
                if k + 1 < level:
                    below_sum[c, k] = total
                    moves[c][k + 1].start()
                else:
                    columns[rows_at_scaled(below_share.shape[0], c * piece, piece)(row)] = total
                    spreads[c].start()
            elif k == level:
                spreads[c].pass_on()
            else:
                spreads[c].finish()

        spread_pivots.pass_on()
        for c in range(chunks):
            moves[c][0].start()
        spread_pivots.finish()
        work[...] = jnp.zeros_like(work)
        for t, (i, j) in enumerate(tiles):
            work[i * BLOCK : (i + 1) * BLOCK, j * BLOCK : (j + 1) * BLOCK] = packed[
                t * BLOCK : (t + 1) * BLOCK
            ]
        if last:
            extra_sum, extra_in0, extra_in1, extra_in2 = take(), take(), take(), take()
            leaf = lax.axis_index("leaf")
            arrivals = [extra_in0, extra_in1, extra_in2]
            heights = [arrival.shape[0] for arrival in arrivals]
            shuffles = []
            for bit in range(LEVELS - 1):
                flag = leaf // 2**bit % 2
                source = extra_in if bit == 0 else extra_sum.at[bit - 1]
                give = source.at[pl.ds(pl.multiple_of((1 - flag) * heights[bit], 8), heights[bit])]
                shuffles.append(remote(give, arrivals[bit], sends, receives, slot, partners[bit]))
                slot += 1

            def shuffle(bit):
                flag = leaf // 2**bit % 2
                shuffles[bit].wait()
                keep = pl.ds(pl.multiple_of(flag * heights[bit], 8), heights[bit])
                source = extra_in if bit == 0 else extra_sum.at[bit - 1]
                total = source[keep] + arrivals[bit][...]
                if bit < LEVELS - 2:
                    extra_sum[bit, : heights[bit]] = total
                    shuffles[bit + 1].start()
                else:
                    extra_sum[bit, : heights[bit]] = total

        plan = {2: [(0, 0)] if level == 1 else [(0, 0), (1, 0)], 3: [(1, 0), (0, 1)] if level == 1 else [(0, 1), (1, 1)]}

        def between(j):
            for when, steps in plan.items():

                @pl.when(j == when)
                def _():
                    for c, k in steps:
                        advance(c, k)
                    if last and when == 2:
                        shuffles[0].start()

        factor(work, factors, between)
        done = [step for steps in plan.values() for step in steps]
        for k in range(level + 2):
            for c in range(chunks):
                if (c, k) not in done:
                    advance(c, k)
            if last and k == level - 1:
                shuffle(0)
        if last:
            shuffle(1)
    solve_below(factors, columns)
    if last:
        shuffle(2)
        height = out.shape[0]
        position = member * row_count + row
        own_rows = columns[pl.ds(pl.multiple_of(position * height, 8), height)]
        out[...] = extra_sum[LEVELS - 2, :height] - dot_nt(own_rows, columns[...])
        return
    width = order // group
    offset = pl.multiple_of(member * width, BLOCK)
    fresh[...] = columns[:, pl.ds(offset, width)]


def share_kernel(level, row_count, front, order, *refs):
    group = 2**level
    below = front - order
    refs = list(refs)
    take = lambda: refs.pop(0)
    inverse_map, next_panel, fresh = take(), take(), take()
    old = take() if level else None
    kept, pivot_out, below_out = take(), take(), take()
    extra = take() if level == LEVELS - 2 else None
    placed, whole_panel, everything = take(), take(), take()
    row = lax.axis_index("row")
    tiles = lower_tiles(order)
    depth = 0 if old is None else old.shape[1]
    width = order // group
    if old is not None:
        kept[:below, :depth] = old[:below]
    kept[:below, depth:] = fresh[...]
    kept[below:] = jnp.zeros((BLOCK, depth + width), jnp.float32)
    for i in range(front // BLOCK):
        block = pl.multiple_of(inverse_map[i] * BLOCK, BLOCK)
        placed[i * BLOCK : (i + 1) * BLOCK] = kept[pl.ds(block, BLOCK)]
    held = next_panel.shape[0]
    whole_panel[...] = jnp.zeros_like(whole_panel)
    place = lax.axis_index("leaf") % (2 * group)
    whole_panel[pl.ds(pl.multiple_of(place * held, 8), held)] = next_panel[...]
    pivots = halves(placed[:order])
    for t, (i, j) in enumerate(tiles):
        down = slice(i * BLOCK, (i + 1) * BLOCK)
        along = slice(j * BLOCK, (j + 1) * BLOCK)
        product = dot_split([p[down] for p in pivots], [p[along] for p in pivots])
        everything[t * BLOCK : (t + 1) * BLOCK] = whole_panel[down, along] - product
    pivot_out[...] = everything[rows_at(pivot_out.shape[0])(row)]
    height = below_out.shape[0]
    mine = rows_at(height, order)(row)
    below_out[...] = whole_panel[mine] - dot_split(halves(placed[mine]), pivots)
    kept[:below] = placed[order:]
    if level == LEVELS - 2:
        top = 2 * group
        height = below // (top * row_count)
        for index in range(top):
            start = pl.multiple_of(order + (index * row_count + row) * height, 8)
            spot = bit_reversed(index, LEVELS - 1)
            placed[spot * height : (spot + 1) * height] = placed[pl.ds(start, height)]
        own_part = halves(placed[: top * height])
        extra[...] = -dot_split(own_part, halves(kept[:below]))


def rows_at_scaled(stride, base, size):
    def place(row):
        return pl.ds(pl.multiple_of(row * stride + base, 8), size)

    return place


def front_step(level, row_count, front, order, operands):
    below = front - order
    width = order // 2**level
    tiles = len(lower_tiles(order))
    share = tiles * BLOCK // row_count
    float32 = jnp.float32

    def vmem(*shape):
        return pltpu.VMEM(shape, float32)

    def out(*shape):
        return jax.ShapeDtypeStruct(shape, float32)

    last = level == LEVELS - 1
    rest = below // row_count
    top = 2 ** (LEVELS - 1)
    gather = row_count - 1
    copies = 3 * gather if level == 0 else 3 * (level + gather) + (LEVELS - 1 if last else 0)
    scratch = [
        vmem(order, order),
        vmem(order, order),
        vmem(below, order),
        pltpu.SemaphoreType.DMA((copies,)),
        pltpu.SemaphoreType.DMA((copies,)),
    ]
    if level == 0:
        scratch.append(vmem(front, order))
    else:
        scratch += [
            vmem(tiles * BLOCK, BLOCK),
            vmem(level, share, BLOCK),
            vmem(level, share, BLOCK),
            vmem(2, level, rest // 2, order),
            vmem(2, level, rest // 2, order),
        ]
    if last:
        scratch += [vmem(LEVELS - 1, rest // 2, below)]
        scratch += [vmem(rest // 2 ** (bit + 1), below) for bit in range(LEVELS - 1)]
        shapes = out(rest // top, below)
    else:
        shapes = out(below, width)
    specs = [pl.BlockSpec(memory_space=pltpu.VMEM)] * len(operands)
    return pl.pallas_call(
        functools.partial(front_kernel, level, row_count, front, order),
        out_shape=shapes,
        in_specs=specs,
        scratch_shapes=scratch,
        name=f"front{level}",
        compiler_params=pltpu.CompilerParams(
            vmem_limit_bytes=60 * 2**20, collective_id=level, has_side_effects=True
        ),
    )(*operands)


def share_step(level, row_count, front, order, operands):
    below = front - order
    depth = sum(order // 2**k for k in range(level + 1))
    tiles = len(lower_tiles(order))
    rest = below // row_count

    def out(*shape):
        return jax.ShapeDtypeStruct(shape, jnp.float32)

    shapes = [out(below + BLOCK, depth), out(tiles * BLOCK // row_count, BLOCK), out(rest, order)]
    if level == LEVELS - 2:
        shapes.append(out(rest, below))
    specs = [pl.BlockSpec(memory_space=pltpu.VMEM)] * len(operands)
    specs[0] = pl.BlockSpec(memory_space=pltpu.SMEM)
    return pl.pallas_call(
        functools.partial(share_kernel, level, row_count, front, order),
        out_shape=shapes,
        in_specs=specs,
        scratch_shapes=[
            pltpu.VMEM((front, depth), jnp.float32),
            pltpu.VMEM((front, order), jnp.float32),
            pltpu.VMEM((tiles * BLOCK, BLOCK), jnp.float32),
        ],
        name=f"share{level}",
        compiler_params=pltpu.CompilerParams(vmem_limit_bytes=60 * 2**20),
    )(*operands)


def body(panel0, panel1, panel2, panel3, maps1, maps2, maps3):
    block_maps = (maps1, maps2, maps3)
    row_count = lax.axis_size("row")
    leaf = lax.axis_index("leaf")
    order = panel0.shape[1]
    front = panel0.shape[0] * row_count
    parents = front // BLOCK
    children = (front - order) // BLOCK
    local = jnp.concatenate([panel1, panel2, panel3], axis=0)
    gathered = lax.all_gather(local, "row", axis=0)
    panels = []
    start = 0
    for panel in (panel1, panel2, panel3):
        rows = panel.shape[0]
        panels.append(gathered[:, start : start + rows].reshape(row_count * rows, order))
        start += rows
    operands = [panel0]
    old = []
    for level in range(LEVELS - 1):
        blocks = lax.dynamic_index_in_dim(block_maps[level], leaf // 2**level, 0, keepdims=False)
        hit = blocks[None, :] == jnp.arange(parents, dtype=jnp.int32)[:, None]
        back = jnp.min(
            jnp.where(hit, jnp.arange(children, dtype=jnp.int32)[None, :], children), axis=1
        )
        fresh = front_step(level, row_count, front, order, operands)
        shared = [back, panels[level], fresh] + old
        result = share_step(level, row_count, front, order, shared)
        old = [result[0]]
        operands = [result[1], result[2]]
    operands.append(result[3])
    return front_step(LEVELS - 1, row_count, front, order, operands)


def solution(mesh):
    rows = P(("leaf", "row"), None)
    return jax.shard_map(
        body,
        mesh=mesh,
        in_specs=(rows, rows, rows, rows, P(), P(), P()),
        out_specs=rows,
        check_vma=False,
    )
```

```python
import functools

import jax
import jax.numpy as jnp
from jax import lax
from jax.experimental import pallas as pl
from jax.experimental.pallas import tpu as pltpu
from jax.sharding import PartitionSpec as P

BLOCK = 128
SUB = 8
LEVELS = 4
CONTRACT_LAST = (((1,), (1,)), ((), ()))


def halves(value):
    high = value.astype(jnp.bfloat16)
    low = (value - high.astype(jnp.float32)).astype(jnp.bfloat16)
    return high, low


def dot_split(left, right):
    left_high, left_low = left
    right_high, right_low = right

    def one(a, b):
        return lax.dot_general(a, b, CONTRACT_LAST, preferred_element_type=jnp.float32)

    return one(left_high, right_high) + (one(left_high, right_low) + one(left_low, right_high))


def dot_nt(left, right):
    return dot_split(halves(left), halves(right))


def spread(value, rows, columns):
    return jnp.broadcast_to(value, (rows, columns))


def diagonal_inverse(block):
    count = BLOCK // SUB
    rows = [block[v * SUB : (v + 1) * SUB] for v in range(count)]
    lane = lax.broadcasted_iota(jnp.int32, (SUB, BLOCK), 1)
    sub = lax.broadcasted_iota(jnp.int32, (SUB, BLOCK), 0)
    for b in range(count):
        base = b * SUB
        inside = (lane >= base) & (lane < base + SUB)
        own = rows[b]
        columns = [spread(own[:, base + j : base + j + 1], SUB, BLOCK) for j in range(SUB)]
        a = [
            [spread(columns[j][i : i + 1], SUB, BLOCK) for j in range(i + 1)] for i in range(SUB)
        ]
        inverse = []
        ratio = [[None] * SUB for _ in range(SUB)]
        for i in range(SUB):
            inverse.append(1.0 / a[i][i])
            for j in range(i + 1, SUB):
                ratio[j][i] = a[j][i] * inverse[i]
            for j in range(i + 1, SUB):
                for k in range(i + 1, j + 1):
                    a[j][k] = a[j][k] - ratio[j][i] * a[k][i]
        cleared = jnp.where(inside, 0.0, own)
        pivots = []
        for j in range(SUB):
            row = spread(cleared[j : j + 1], SUB, BLOCK)
            row = jnp.where(lane == base + j, 1.0, row)
            for i in range(j):
                row = row - ratio[j][i] * pivots[i]
            pivots.append(row)
        for v in range(b + 1, count):
            old = rows[v]
            new = jnp.where(inside, 0.0, old)
            factors = []
            for j in range(SUB):
                column = spread(old[:, base + j : base + j + 1], SUB, BLOCK)
                for i in range(j):
                    column = column - factors[i] * a[j][i]
                factors.append(column * inverse[j])
            for j in range(SUB):
                new = new - factors[j] * pivots[j]
            rows[v] = new
        final = jnp.zeros((SUB, BLOCK), jnp.float32)
        scale = jnp.ones((SUB, BLOCK), jnp.float32)
        for j in range(SUB):
            final = jnp.where(sub == j, pivots[j], final)
            scale = jnp.where(sub == j, a[j][j], scale)
        rows[b] = jnp.where(lane <= sub + base, final / jnp.sqrt(scale), 0.0)
    return jnp.concatenate(rows, axis=0)


def factor(work, out, between):
    order = work.shape[0]
    tiles = order // BLOCK
    row_ids = lax.broadcasted_iota(jnp.int32, (order, BLOCK), 0)

    def step(j, carry):
        between(j)
        start = pl.multiple_of(j * BLOCK, BLOCK)
        span = pl.ds(start, BLOCK)
        inverse = diagonal_inverse(work[span, span])

        @pl.when(j == tiles - 1)
        def _():
            out[span, span] = inverse

        @pl.when(j < tiles - 1)
        def _():
            below = jnp.where(row_ids >= start + BLOCK, work[:, span], 0.0)
            column = dot_nt(below, inverse)
            out[:, span] = column
            out[span, span] = inverse
            pieces = halves(column)
            work[...] = work[...] - dot_split(pieces, pieces)

        return carry

    lax.fori_loop(0, tiles, step, 0)


def solve_below(factors, columns):
    order = factors.shape[0]
    for j in range(order // BLOCK):
        span = slice(j * BLOCK, (j + 1) * BLOCK)
        value = columns[:, span]
        if j:
            value = value - dot_nt(columns[:, : j * BLOCK], factors[span, : j * BLOCK])
        columns[:, span] = dot_nt(value, factors[span, span])


def neighbours(level):
    leaf = lax.axis_index("leaf")
    row = lax.axis_index("row")
    partners = []
    for bit in range(level):
        flag = leaf // 2**bit % 2
        partners.append({"leaf": leaf + (1 - 2 * flag) * 2**bit, "row": row})
    count = lax.axis_size("row")
    sibling = row + 1 - 2 * (row % 2)
    forward = [lax.rem(row + 2 * d, count) for d in range(1, count // 2)]
    backward = [lax.rem(row + count - 2 * d, count) for d in range(1, count // 2)]
    across = [{"leaf": leaf, "row": other} for other in forward]
    return partners, {"leaf": leaf, "row": sibling}, across, backward


def remote(source, target, sends, receives, slot, device):
    return pltpu.make_async_remote_copy(
        src_ref=source,
        dst_ref=target,
        send_sem=sends.at[slot],
        recv_sem=receives.at[slot],
        device_id=device,
        device_id_type=pl.DeviceIdType.MESH,
    )


class Gather:
    def __init__(self, buffer, place, sends, receives, slot, near, source=None):
        _, sibling, across, origins = near
        own = buffer.at[place(lax.axis_index("row"))]
        if source is None:
            source = own
        self.direct = remote(source, own, sends, receives, slot, sibling)
        self.far = []
        self.relay = []
        for n, (device, origin) in enumerate(zip(across, origins)):
            self.far.append(remote(source, own, sends, receives, slot + 1 + 2 * n, device))
            passed = buffer.at[place(origin)]
            self.relay.append(remote(passed, passed, sends, receives, slot + 2 + 2 * n, sibling))

    def start(self):
        for copy in self.far:
            copy.start()
        self.direct.start()

    def pass_on(self):
        for copy, relay in zip(self.far, self.relay):
            copy.wait_recv()
            relay.start()

    def finish(self):
        self.direct.wait_recv()
        for relay in self.relay:
            relay.wait_recv()
        for copy in [self.direct] + self.far + self.relay:
            copy.wait_send()


def rows_at(size, base=0):
    def place(row):
        return pl.ds(pl.multiple_of(row * size + base, 8), size)

    return place


def lower_tiles(order):
    return [(i, j) for i in range(order // BLOCK) for j in range(i + 1)]


def entry_barrier(near):
    partners, sibling, across, _ = near
    barrier = pltpu.get_barrier_semaphore()
    peers = partners + [sibling] + across
    for peer in peers:
        pl.semaphore_signal(barrier, inc=1, device_id=peer, device_id_type=pl.DeviceIdType.MESH)
    pl.semaphore_wait(barrier, len(peers))


def bit_reversed(index, bits):
    return sum((index >> b & 1) << (bits - 1 - b) for b in range(bits))


def front_kernel(level, row_count, front, order, *refs):
    last = level == LEVELS - 1
    first = level == 0
    group = 2**level
    below = front - order
    refs = list(refs)
    take = lambda: refs.pop(0)
    row = lax.axis_index("row")
    member = lax.axis_index("leaf") % group
    if first:
        panel, *later = [take() for _ in range(LEVELS)]
    else:
        pivot_share, below_share = take(), take()
    if last:
        extra_in = take()
        out = take()
    else:
        fresh = take()
        joined = [take() for _ in range(LEVELS - 1)] if first else []
    work, factors, columns, sends, receives = take(), take(), take(), take(), take()
    near = neighbours(level)
    partners = near[0]
    tiles = lower_tiles(order)
    entry_barrier(near)
    if first:
        gathered, *held = [take() for _ in range(LEVELS)]
        chunk = panel.shape[0]
        pieces = 3
        size = chunk // pieces
        own = pl.ds(pl.multiple_of(row * chunk, 8), chunk)
        gathered[own] = panel[...]
        moves = []
        for c in range(pieces):
            moves.append(
                Gather(
                    gathered,
                    rows_at_scaled(chunk, c * size, size),
                    sends,
                    receives,
                    (row_count - 1) * c,
                    near,
                    panel.at[pl.ds(c * size, size)],
                )
            )
        for move in moves:
            move.start()
        for move in moves:
            move.pass_on()
        for move in moves:
            move.finish()
        work[...] = gathered[:order]
        columns[...] = gathered[order:]
        slot = (row_count - 1) * pieces
        for part, buffer in zip(later, held):
            size = part.shape[0]
            buffer[rows_at(size)(row)] = part[...]
            moves.append(Gather(buffer, rows_at(size), sends, receives, slot, near, part))
            slot += row_count - 1
            moves[-1].start()
        early = moves[pieces:]

        def between(j):
            @pl.when(j == 3)
            def _():
                for move in early:
                    move.pass_on()

        factor(work, factors, between)
    else:
        packed, pivot_sum, pivot_in, below_sum, below_in = take(), take(), take(), take(), take()
        share = pivot_share.shape[0]
        mine = rows_at(share)(row)
        slot = 0
        source = pivot_share
        for bit in range(level):
            move = remote(source, pivot_in.at[bit], sends, receives, slot, partners[bit])
            slot += 1
            move.start()
            move.wait()
            total = source[...] + pivot_in[bit]
            if bit + 1 < level:
                pivot_sum[bit] = total
                source = pivot_sum.at[bit]
            else:
                packed[mine] = total
        spread_pivots = Gather(packed, rows_at(share), sends, receives, slot, near)
        slot += row_count - 1
        spread_pivots.start()
        chunks = 2
        piece = below_share.shape[0] // chunks
        orders = [list(range(level)), list(range(level))]
        if level > 1:
            orders[1][0], orders[1][1] = 1, 0
        moves = [[None] * level for _ in range(chunks)]
        spreads = []
        for c in range(chunks):
            for k in range(level):
                source = below_share.at[pl.ds(c * piece, piece)] if k == 0 else below_sum.at[c, k - 1]
                moves[c][k] = remote(
                    source, below_in.at[c, k], sends, receives, slot, partners[orders[c][k]]
                )
                slot += 1
            spreads.append(
                Gather(columns, rows_at_scaled(below_share.shape[0], c * piece, piece), sends, receives, slot, near)
            )
            slot += row_count - 1

        def advance(c, k):
            if k < level:
                moves[c][k].wait()
                if k == 0:
                    total = below_share[c * piece : (c + 1) * piece] + below_in[c, 0]
                else:
                    total = below_sum[c, k - 1] + below_in[c, k]
                if k + 1 < level:
                    below_sum[c, k] = total
                    moves[c][k + 1].start()
                else:
                    columns[rows_at_scaled(below_share.shape[0], c * piece, piece)(row)] = total
                    spreads[c].start()
            elif k == level:
                spreads[c].pass_on()
            else:
                spreads[c].finish()

        spread_pivots.pass_on()
        for c in range(chunks):
            moves[c][0].start()
        spread_pivots.finish()
        work[...] = jnp.zeros_like(work)
        for t, (i, j) in enumerate(tiles):
            work[i * BLOCK : (i + 1) * BLOCK, j * BLOCK : (j + 1) * BLOCK] = packed[
                t * BLOCK : (t + 1) * BLOCK
            ]
        if last:
            extra_sum, extra_in0, extra_in1, extra_in2 = take(), take(), take(), take()
            leaf = lax.axis_index("leaf")
            arrivals = [extra_in0, extra_in1, extra_in2]
            heights = [arrival.shape[0] for arrival in arrivals]
            shuffles = []
            for bit in range(LEVELS - 1):
                flag = leaf // 2**bit % 2
                source = extra_in if bit == 0 else extra_sum.at[bit - 1]
                give = source.at[pl.ds(pl.multiple_of((1 - flag) * heights[bit], 8), heights[bit])]
                shuffles.append(remote(give, arrivals[bit], sends, receives, slot, partners[bit]))
                slot += 1

            def shuffle(bit):
                flag = leaf // 2**bit % 2
                shuffles[bit].wait()
                keep = pl.ds(pl.multiple_of(flag * heights[bit], 8), heights[bit])
                source = extra_in if bit == 0 else extra_sum.at[bit - 1]
                total = source[keep] + arrivals[bit][...]
                if bit < LEVELS - 2:
                    extra_sum[bit, : heights[bit]] = total
                    shuffles[bit + 1].start()
                else:
                    extra_sum[bit, : heights[bit]] = total

        plan = {2: [(0, 0)] if level == 1 else [(0, 0), (1, 0)], 3: [(1, 0), (0, 1)] if level == 1 else [(0, 1), (1, 1)]}

        def between(j):
            for when, steps in plan.items():

                @pl.when(j == when)
                def _():
                    for c, k in steps:
                        advance(c, k)
                    if last and when == 2:
                        shuffles[0].start()

        factor(work, factors, between)
        done = [step for steps in plan.values() for step in steps]
        for k in range(level + 2):
            for c in range(chunks):
                if (c, k) not in done:
                    advance(c, k)
            if last and k == level - 1:
                shuffle(0)
        if last:
            shuffle(1)
    solve_below(factors, columns)
    if last:
        shuffle(2)
        height = out.shape[0]
        position = member * row_count + row
        own_rows = columns[pl.ds(pl.multiple_of(position * height, 8), height)]
        out[...] = extra_sum[LEVELS - 2, :height] - dot_nt(own_rows, columns[...])
        return
    width = order // group
    offset = pl.multiple_of(member * width, BLOCK)
    fresh[...] = columns[:, pl.ds(offset, width)]
    if first:
        for move, buffer, target in zip(early, held, joined):
            move.finish()
            target[...] = buffer[...]


def share_kernel(level, row_count, front, order, *refs):
    group = 2**level
    below = front - order
    refs = list(refs)
    take = lambda: refs.pop(0)
    inverse_map, next_panel, fresh = take(), take(), take()
    old = take() if level else None
    kept, pivot_out, below_out = take(), take(), take()
    extra = take() if level == LEVELS - 2 else None
    placed, whole_panel, everything = take(), take(), take()
    row = lax.axis_index("row")
    tiles = lower_tiles(order)
    depth = 0 if old is None else old.shape[1]
    width = order // group
    if old is not None:
        kept[:below, :depth] = old[:below]
    kept[:below, depth:] = fresh[...]
    kept[below:] = jnp.zeros((BLOCK, depth + width), jnp.float32)
    for i in range(front // BLOCK):
        block = pl.multiple_of(inverse_map[i] * BLOCK, BLOCK)
        placed[i * BLOCK : (i + 1) * BLOCK] = kept[pl.ds(block, BLOCK)]
    held = next_panel.shape[0]
    whole_panel[...] = jnp.zeros_like(whole_panel)
    place = lax.axis_index("leaf") % (2 * group)
    whole_panel[pl.ds(pl.multiple_of(place * held, 8), held)] = next_panel[...]
    pivots = halves(placed[:order])
    for t, (i, j) in enumerate(tiles):
        down = slice(i * BLOCK, (i + 1) * BLOCK)
        along = slice(j * BLOCK, (j + 1) * BLOCK)
        product = dot_split([p[down] for p in pivots], [p[along] for p in pivots])
        everything[t * BLOCK : (t + 1) * BLOCK] = whole_panel[down, along] - product
    pivot_out[...] = everything[rows_at(pivot_out.shape[0])(row)]
    height = below_out.shape[0]
    mine = rows_at(height, order)(row)
    below_out[...] = whole_panel[mine] - dot_split(halves(placed[mine]), pivots)
    kept[:below] = placed[order:]
    if level == LEVELS - 2:
        top = 2 * group
        height = below // (top * row_count)
        for index in range(top):
            start = pl.multiple_of(order + (index * row_count + row) * height, 8)
            spot = bit_reversed(index, LEVELS - 1)
            placed[spot * height : (spot + 1) * height] = placed[pl.ds(start, height)]
        own_part = halves(placed[: top * height])
        extra[...] = -dot_split(own_part, halves(kept[:below]))


def rows_at_scaled(stride, base, size):
    def place(row):
        return pl.ds(pl.multiple_of(row * stride + base, 8), size)

    return place


def front_step(level, row_count, front, order, operands):
    below = front - order
    width = order // 2**level
    tiles = len(lower_tiles(order))
    share = tiles * BLOCK // row_count
    float32 = jnp.float32

    def vmem(*shape):
        return pltpu.VMEM(shape, float32)

    def out(*shape):
        return jax.ShapeDtypeStruct(shape, float32)

    last = level == LEVELS - 1
    rest = below // row_count
    top = 2 ** (LEVELS - 1)
    gather = row_count - 1
    copies = (LEVELS + 2) * gather if level == 0 else 3 * (level + gather) + (LEVELS - 1 if last else 0)
    scratch = [
        vmem(order, order),
        vmem(order, order),
        vmem(below, order),
        pltpu.SemaphoreType.DMA((copies,)),
        pltpu.SemaphoreType.DMA((copies,)),
    ]
    if level == 0:
        scratch.append(vmem(front, order))
        heights = [row_count * operand.shape[0] for operand in operands[1:]]
        scratch += [vmem(height, order) for height in heights]
    else:
        scratch += [
            vmem(tiles * BLOCK, BLOCK),
            vmem(level, share, BLOCK),
            vmem(level, share, BLOCK),
            vmem(2, level, rest // 2, order),
            vmem(2, level, rest // 2, order),
        ]
    if last:
        scratch += [vmem(LEVELS - 1, rest // 2, below)]
        scratch += [vmem(rest // 2 ** (bit + 1), below) for bit in range(LEVELS - 1)]
        shapes = out(rest // top, below)
    else:
        shapes = [out(below, width)]
        if level == 0:
            shapes += [out(height, order) for height in heights]
    specs = [pl.BlockSpec(memory_space=pltpu.VMEM)] * len(operands)
    return pl.pallas_call(
        functools.partial(front_kernel, level, row_count, front, order),
        out_shape=shapes,
        in_specs=specs,
        scratch_shapes=scratch,
        name=f"front{level}",
        compiler_params=pltpu.CompilerParams(
            vmem_limit_bytes=60 * 2**20, collective_id=level, has_side_effects=True
        ),
    )(*operands)


def share_step(level, row_count, front, order, operands):
    below = front - order
    depth = sum(order // 2**k for k in range(level + 1))
    tiles = len(lower_tiles(order))
    rest = below // row_count

    def out(*shape):
        return jax.ShapeDtypeStruct(shape, jnp.float32)

    shapes = [out(below + BLOCK, depth), out(tiles * BLOCK // row_count, BLOCK), out(rest, order)]
    if level == LEVELS - 2:
        shapes.append(out(rest, below))
    specs = [pl.BlockSpec(memory_space=pltpu.VMEM)] * len(operands)
    specs[0] = pl.BlockSpec(memory_space=pltpu.SMEM)
    return pl.pallas_call(
        functools.partial(share_kernel, level, row_count, front, order),
        out_shape=shapes,
        in_specs=specs,
        scratch_shapes=[
            pltpu.VMEM((front, depth), jnp.float32),
            pltpu.VMEM((front, order), jnp.float32),
            pltpu.VMEM((tiles * BLOCK, BLOCK), jnp.float32),
        ],
        name=f"share{level}",
        compiler_params=pltpu.CompilerParams(vmem_limit_bytes=60 * 2**20),
    )(*operands)


def body(panel0, panel1, panel2, panel3, maps1, maps2, maps3):
    block_maps = (maps1, maps2, maps3)
    row_count = lax.axis_size("row")
    leaf = lax.axis_index("leaf")
    order = panel0.shape[1]
    front = panel0.shape[0] * row_count
    parents = front // BLOCK
    children = (front - order) // BLOCK
    operands = [panel0, panel1, panel2, panel3]
    old = []
    panels = []
    for level in range(LEVELS - 1):
        blocks = lax.dynamic_index_in_dim(block_maps[level], leaf // 2**level, 0, keepdims=False)
        hit = blocks[None, :] == jnp.arange(parents, dtype=jnp.int32)[:, None]
        back = jnp.min(
            jnp.where(hit, jnp.arange(children, dtype=jnp.int32)[None, :], children), axis=1
        )
        fresh, *joined = front_step(level, row_count, front, order, operands)
        panels = joined or panels
        shared = [back, panels[level], fresh] + old
        result = share_step(level, row_count, front, order, shared)
        old = [result[0]]
        operands = [result[1], result[2]]
    operands.append(result[3])
    return front_step(LEVELS - 1, row_count, front, order, operands)


def solution(mesh):
    rows = P(("leaf", "row"), None)
    return jax.shard_map(
        body,
        mesh=mesh,
        in_specs=(rows, rows, rows, rows, P(), P(), P()),
        out_specs=rows,
        check_vma=False,
    )
```
